768 devices in a mesh: col: 192 (over z, y, x_lo), row: 4 (over x_hi, core).
Axes of the slice: x: 4 (x_hi: 2, x_lo: 2; x = x_hi * 2 + x_lo), y: 8, z: 12, core: 2. Of those that a mesh axis runs over, the one named last changes fastest.
Arguments:
- pivot_block: bfloat16 [512, 512], P(None, 'row'), may hold values from -0.5 to 5.5, as said below
- panel: bfloat16 [4, 6144, 512], P('row', 'col'), may hold values from -1.1953125 to 1.1953125
- lead: int32 [4, 48], P('row'), may hold values from 0 to 3
- trailing: bfloat16 [24576, 24576], P('row', 'col'), may hold values from -1.796875 to 1.796875
Outputs:
- pivot_factor: float32 [512, 512], P(None, 'row')
- panel_factor: bfloat16 [4, 6144, 512], P('row', 'col')
- schur: bfloat16 [24576, 24576], P('row', 'col')
The draws below stay inside these ranges and needn't reach their ends.
Inputs may be any that keep to these rules, and one draw needn't show every extreme that they name: `pivot_block`: symmetric positive definite.
All inputs are finite; a program needn't handle non-finite values.
Results may differ from the reference program's by a relative error of at most 0.0042.
Values may be sent and summed in bfloat16 or wider, within the bound.
A program may use at most 32 MiB of HBM per device.

```python
import math
import jax
import jax.numpy as jnp
from jax import lax

PIVOT = 512
BLOCK = 128
KB = 4
GROUPS = 4
GROUP_ROWS = 6144
GROUP_BLOCKS = 48
TRAIL = 24576


def draw_pivot_block(key, part):
    first_key, second_key, third_key = jax.random.split(jax.random.fold_in(key, 11), 3)
    position = jnp.arange(PIVOT).astype(jnp.float32)
    distance = jnp.abs(position[:, None] - position[None, :])
    length_scale = PIVOT / 16.0
    kernel = jnp.exp(-distance / length_scale)
    scales = jnp.exp(jax.random.uniform(first_key, (PIVOT,), jnp.float32, math.log(0.75), math.log(1.25)))
    jitter = jax.random.normal(second_key, (PIVOT, PIVOT), jnp.float32) * 0.02
    symmetric = jnp.clip((jitter + jitter.T) * 0.5, -0.06, 0.06)
    diagonal = jax.random.uniform(third_key, (PIVOT,), jnp.float32, 2.0, 3.0)
    correlated = 1.5 * kernel * scales[:, None] * scales[None, :]
    return (correlated + symmetric + jnp.eye(PIVOT, dtype=jnp.float32) * diagonal[None, :]).astype(jnp.bfloat16)


def draw_lead(key, part):
    first_key, second_key = jax.random.split(jax.random.fold_in(key, 23))
    earliest = jax.random.randint(first_key, (GROUPS, 1), 0, KB // 2)
    return jax.random.randint(second_key, (GROUPS, GROUP_BLOCKS), earliest, KB).astype(jnp.int32)


def steps_of(stream_key, dims, shards, least, high):
    def one(dim, shards_of):
        steps = jax.random.uniform(jax.random.fold_in(jax.random.fold_in(stream_key, 6), dim), (shards_of,), jnp.float32, least / len(shards), high / len(shards))
        return jnp.repeat(jnp.exp(steps), dims[dim] // shards_of).reshape((-1,) + (1,) * (len(dims) - dim - 1))

    gain = one(*shards[0])
    for cut in shards[1:]:
        gain = gain * one(*cut)
    return gain


def gaussian(stream_key, shape, width, reach, pieces=(), kind=jnp.bfloat16):
    entries = jax.random.normal(stream_key, shape, jnp.float32) * width
    if len(pieces) > 0:
        entries = steps_of(stream_key, shape, pieces, -0.22, 0.18) * entries
    return jnp.clip(entries, min=-reach, max=reach).astype(kind)


def setup_inputs(seed: int = 0) -> dict:
    seeds = jax.random.split(jax.random.key(seed), 5)
    pivot_block = draw_pivot_block(jax.random.fold_in(seeds[4], 71), 0)
    panel = gaussian(seeds[1], (GROUPS, GROUP_ROWS, PIVOT), 0.2, 1.1953125, ((0, 4), (1, 192)))
    lead = draw_lead(jax.random.fold_in(seeds[4], 71), 0)
    trailing = gaussian(seeds[3], (TRAIL, TRAIL), 0.3, 1.796875, ((0, 4), (1, 192)))
    return dict(pivot_block=pivot_block, panel=panel, lead=lead, trailing=trailing)


def reference(pivot_block, panel, lead, trailing):
    pivot_factor = jnp.linalg.cholesky(pivot_block.astype(jnp.float32))
    col_block = (jnp.arange(PIVOT) // BLOCK).astype(jnp.int32)
    row_lead = jnp.repeat(lead, BLOCK, axis=1)
    live_mask = col_block[None, None, :] >= row_lead[:, :, None]
    masked = jnp.where(live_mask, panel.astype(jnp.float32), jnp.float32(0.0)).reshape(TRAIL, PIVOT)
    solved = jax.scipy.linalg.solve_triangular(pivot_factor, masked.T, lower=True).T
    panel_factor = solved.astype(jnp.bfloat16)
    panel_wide = panel_factor.astype(jnp.float32)

    def one_group(group_index):
        first = (group_index * GROUP_ROWS).astype(jnp.int32)
        group_rows = lax.dynamic_slice_in_dim(panel_wide, first, GROUP_ROWS, 0)
        target_rows = lax.dynamic_slice_in_dim(trailing, first, GROUP_ROWS, 0)
        update = jnp.dot(group_rows, panel_wide.T, precision=lax.Precision.HIGHEST)
        return (target_rows.astype(jnp.float32) - update).astype(jnp.bfloat16)
    schur = lax.map(one_group, jnp.arange(GROUPS).astype(jnp.int32)).reshape(TRAIL, TRAIL)
    return (pivot_factor, panel_factor.reshape(GROUPS, GROUP_ROWS, PIVOT), schur)
```

```python
import functools
import heapq

import jax
import jax.numpy as jnp
from jax import lax
from jax.experimental import pallas as pl
from jax.experimental.pallas import tpu as pltpu
from jax.sharding import PartitionSpec as P

F32 = jnp.float32
BF = jnp.bfloat16
MESH = pl.DeviceIdType.MESH
NZ, NY, NX, NR = 12, 8, 2, 4
NC = NZ * NY * NX
HALF = 256
POINTS = 8


def split(a):
    hi = a.astype(BF)
    return hi, (a - hi.astype(F32)).astype(BF)


def dot3(a, b, ca, cb):
    ah, al = split(a)
    bh, bl = split(b)
    d = functools.partial(
        lax.dot_general,
        dimension_numbers=(((ca,), (cb,)), ((), ())),
        preferred_element_type=F32,
    )
    return d(ah, bh) + (d(ah, bl) + d(al, bh))


def lane_b(x, j):
    return jnp.broadcast_to(x[:, j : j + 1], (8, 128))


def sub_b(x, i):
    return jnp.broadcast_to(x[i : i + 1, :], (8, 128))


def factor128(slabs, at):
    lane = lax.broadcasted_iota(jnp.int32, (8, 128), 1)
    sub = lax.broadcasted_iota(jnp.int32, (8, 128), 0)
    S = list(slabs)
    V = [jnp.where(lane == sub + 8 * p, F32(1.0), F32(0.0)) for p in range(16)]
    Us, Vs = [], []

    def gather_rows(rows):
        x = rows[0]
        for i in range(1, 8):
            x = jnp.where(sub == i, rows[i], x)
        return x

    for p in range(16):
        at(p)
        Sp, Vp = S[p], V[p]
        C = [lane_b(Sp, 8 * p + j) for j in range(8)]
        e = [[sub_b(C[j], i) for j in range(8)] for i in range(8)]
        r = [sub_b(Sp, i) for i in range(8)]
        v = [sub_b(Vp, i) for i in range(8)]
        d, ur, vr = [], [], []
        for j in range(8):
            inv = 1.0 / e[j][j]
            d.append(e[j][j])
            ur.append(r[j])
            vr.append(v[j])
            rj, vj = r[j] * inv, v[j] * inv
            ej = [e[j][m] * inv if m > j else None for m in range(8)]
            for i in range(8):
                if i != j:
                    f = e[i][j]
                    for m in range(j + 1, 8):
                        e[i][m] = e[i][m] - f * ej[m]
                    r[i] = r[i] - f * rj
                    v[i] = v[i] - f * vj
            r[j], v[j] = rj, vj
            for m in range(j + 1, 8):
                e[j][m] = ej[m]
        for q in range(p + 1, 16):
            T = [lane_b(S[q], 8 * p + j) for j in range(8)]
            a = [T[j] * r[j] for j in range(8)]
            b = [T[j] * v[j] for j in range(8)]
            while len(a) > 1:
                a = [a[i] + a[i + 1] for i in range(0, len(a), 2)]
                b = [b[i] + b[i + 1] for i in range(0, len(b), 2)]
            S[q] = S[q] - a[0]
            V[q] = V[q] - b[0]
        rs = lax.rsqrt(gather_rows(d))
        Us.append(jnp.where(lane >= sub + 8 * p, gather_rows(ur) * rs, F32(0.0)))
        Vs.append(gather_rows(vr) * rs)
    return Us, Vs


def plan():
    size = {"z": NZ, "y": NY}

    def children(half, dz, dy):
        last, first = ("y", "z") if half == 0 else ("z", "y")
        pos = {"z": dz, "y": dy}
        out = []

        def step(axis, sign):
            n = size[axis]
            other = pos["z" if axis == "y" else "y"]
            reach = n // 2
            if n % 2 == 0:
                plus = other % 2 == 0
                reach = n // 2 if plus == (sign > 0) else n // 2 - 1
            new = pos[axis] + sign
            if abs(new) <= reach:
                q = dict(pos)
                q[axis] = new
                out.append((axis, sign, (half, q["z"], q["y"])))

        if pos[last] == 0:
            for sign in (1, -1):
                if pos[first] == 0 or (pos[first] > 0) == (sign > 0):
                    step(first, sign)
            for sign in (1, -1):
                step(last, sign)
        else:
            step(last, 1 if pos[last] > 0 else -1)
        return out

    free = {}
    heap = [(2.0, 0, (0, 0, 0)), (2.0, 1, (1, 0, 0))]
    order = []
    count = 2
    while heap:
        t, _, msg = heapq.heappop(heap)
        kids = children(*msg)
        order.append((t, msg, kids))
        for axis, sign, kid in kids:
            start = max(t, free.get((axis, sign), 0.0))
            free[(axis, sign)] = start + 0.72
            heapq.heappush(heap, (start + 0.72 + 1.6, count, kid))
            count += 1
    return order


def gather_factor(m_ref, piv_ref, G, U, V, A, PV, bar_x, sem_x, sem_r, sem_s, sem_l, sem_p, sem_ps):
    col, row = lax.axis_index("col"), lax.axis_index("row")
    z, y, x = col // (NY * NX), (col // NX) % NY, col % NX

    def at_col(zz, yy, xx):
        return (zz * NY + yy) * NX + xx

    def wrap(v, n):
        return lax.rem(v + n, n)

    x_nbr = at_col(z, y, 1 - x)
    hop = {
        ("z", 1): at_col(wrap(z + 1, NZ), y, x),
        ("z", -1): at_col(wrap(z - 1, NZ), y, x),
        ("y", 1): at_col(z, wrap(y + 1, NY), x),
        ("y", -1): at_col(z, wrap(y - 1, NY), x),
    }
    own = []
    for half in range(2):
        own.append(pltpu.make_async_copy(m_ref.at[pl.ds(half, 1)], G.at[pl.ds(half * NC + col, 1)], sem_l.at[half]))
        own[half].start()
    for i in range(4):

        @pl.when(row >= i)
        def _():
            pltpu.make_async_copy(
                piv_ref.at[pl.ds(128 * i, 128)], PV.at[row, pl.ds(128 * i, 128)], sem_p.at[row, i]
            ).start()

    barrier = pltpu.get_barrier_semaphore()
    for c in [x_nbr] + list(hop.values()):
        pl.semaphore_signal(barrier, inc=1, device_id=(c, row), device_id_type=MESH)
    for k in range(1, 4):
        pl.semaphore_signal(barrier, inc=1, device_id=(col, lax.rem(row + k, 4)), device_id_type=MESH)
    pl.semaphore_wait(barrier, 8)

    for i in range(4):

        @pl.when(row >= i)
        def _():
            for k in range(1, 4):
                pltpu.make_async_remote_copy(
                    src_ref=piv_ref.at[pl.ds(128 * i, 128)],
                    dst_ref=PV.at[row, pl.ds(128 * i, 128)],
                    send_sem=sem_ps.at[k - 1, i],
                    recv_sem=sem_p.at[row, i],
                    device_id=(col, lax.rem(row + k, 4)),
                    device_id_type=MESH,
                ).start()

    xs = []
    for half in range(2):
        xs.append(
            pltpu.make_async_remote_copy(
                src_ref=m_ref.at[pl.ds(half, 1)],
                dst_ref=G.at[pl.ds(half * NC + col, 1)],
                send_sem=sem_x.at[half],
                recv_sem=bar_x.at[half],
                device_id=(x_nbr, row),
                device_id_type=MESH,
            )
        )
        xs[half].start()

    events = plan()
    index = {msg: i for i, (_, msg, _) in enumerate(events)}

    def pair(msg):
        half, dz, dy = msg
        zz, yy = wrap(z - dz, NZ), wrap(y - dy, NY)
        return G.at[pl.ds(half * NC + (zz * NY + yy) * NX, 2)]

    def handle(event):
        _, msg, kids = event
        half, dz, dy = msg
        ref = pair(msg)
        if dz == 0 and dy == 0:
            own[half].wait()
            xs[half].wait()
        else:
            pltpu.make_async_copy(ref, ref, sem_r.at[index[msg]]).wait()
        for axis, sign, kid in kids:
            pltpu.make_async_remote_copy(
                src_ref=ref,
                dst_ref=ref,
                send_sem=sem_s.at[0],
                recv_sem=sem_r.at[index[kid]],
                device_id=(hop[(axis, sign)], row),
                device_id_type=MESH,
            ).start()

    def wait_piv(s, i):
        ref = PV.at[s, pl.ds(128 * i, 128)]
        pltpu.make_async_copy(ref, ref, sem_p.at[s, i]).wait()
        A[pl.ds(128 * i, 128), pl.ds(128 * s, 128)] = PV[s, pl.ds(128 * i, 128), :].astype(F32)

    t0, dt = 1.0, 7.0 / POINTS
    when_ = {}
    late = []
    for ev in events:
        slot = max(0, int((ev[0] + 0.5 - t0) / dt) + 1)
        if slot < 4 * POINTS:
            when_.setdefault(slot, []).append(ev)
        else:
            late.append(ev)

    wait_piv(0, 0)
    for k in range(4):
        o = 128 * k

        def at(p):
            if p % (16 // POINTS) == 0:
                for ev in when_.get(k * POINTS + p // (16 // POINTS), []):
                    handle(ev)

        D = A[o : o + 128, o : o + 128]
        Us, Vs = factor128([D[8 * p : 8 * p + 8] for p in range(16)], at)
        Vk = jnp.concatenate(Vs, axis=0)
        V[k] = Vk
        U[o : o + 128, o : o + 128] = jnp.concatenate(Us, axis=0)
        if k > 0:
            U[o : o + 128, 0:o] = jnp.zeros((128, o), F32)
        if k == 0:
            for s in range(1, 4):
                for i in range(s + 1):
                    wait_piv(s, i)
        if k < 3:
            rest = dot3(Vk, A[o : o + 128, o + 128 :], 1, 0)
            U[o : o + 128, o + 128 :] = rest
            for i in range(k + 1, 4):
                b = 128 * (i - k - 1)
                A[128 * i : 128 * i + 128, 128 * i :] -= dot3(rest[:, b : b + 128], rest[:, b:], 0, 0)
    for ev in late:
        handle(ev)
    sent = sum(len(kids) for _, _, kids in events)
    ref = G.at[pl.ds(0, 2 * sent)]
    pltpu.make_async_copy(ref, ref, sem_s.at[0]).wait()
    for i in range(4):

        @pl.when(row >= i)
        def _():
            for k in range(1, 4):
                src = piv_ref.at[pl.ds(128 * i, 128)]
                pltpu.make_async_copy(src, src, sem_ps.at[k - 1, i]).wait()


def update(g_ref, t_ref, mc_ref, m_ref, U, V, s_ref, p_ref, l_ref, Z):
    row = lax.axis_index("row")

    @pl.when(pl.program_id(0) == 0)
    def _():
        pieces = [mc_ref[lax.rem(row - j + 4, 4)] for j in range(4)]
        rows = jnp.concatenate(pieces + [jnp.concatenate([m_ref[0], m_ref[1]], axis=1)], axis=0)
        xs = [None] * 4
        rhs = [rows[:, 128 * k : 128 * k + 128].astype(F32) for k in range(4)]
        for k in range(4):
            xs[k] = dot3(rhs[k], V[k], 1, 1)
            for i in range(k + 1, 4):
                rhs[i] = rhs[i] - dot3(xs[k], U[128 * k : 128 * k + 128, 128 * i : 128 * i + 128], 1, 0)
        p_ref[...] = jnp.concatenate([a[128:160] for a in xs], axis=1).astype(BF)
        back = [a[:128] for a in xs]
        for k in range(3, -1, -1):
            zk = dot3(back[k], V[k], 1, 0)
            hi, lo = split(zk)
            Z[0:128, 128 * k : 128 * k + 128] = hi
            Z[128:256, 128 * k : 128 * k + 128] = lo
            for i in range(k):
                back[i] = back[i] - dot3(zk, U[128 * i : 128 * i + 128, 128 * k : 128 * k + 128], 1, 1)
        o = pl.multiple_of(row * 128, 128)
        l_ref[...] = U[pl.ds(o, 128), :].T

    dims = (((1,), (1,)), ((), ()))
    acc = lax.dot_general(g_ref[0], Z[:, 0:HALF], dims, preferred_element_type=F32)
    acc = acc + lax.dot_general(g_ref[1], Z[:, HALF:], dims, preferred_element_type=F32)
    s_ref[...] = (t_ref[...].astype(F32) - (acc[:, 0:128] + acc[:, 128:256])).astype(BF)


def body(pivot_block, panel, lead, trailing):
    col, row = lax.axis_index("col"), lax.axis_index("row")
    own_lead = lax.dynamic_slice(lead, (0, col // 4), (1, 1))[0, 0]
    block = jnp.arange(512) // 128
    masked = jnp.where((block >= own_lead)[None, :], panel[0], jnp.zeros((), BF))
    halves = masked.reshape(32, 2, HALF).transpose(1, 0, 2)

    pieces = []
    for m in range(4):
        perm = []
        for g in range(4):
            for c in range(NC):
                u, j = c // 4, c % 4
                perm.append((c * NR + g, (48 * g + u) * NR + (j + m) % 4))
        pieces.append(lax.ppermute(masked, ("col", "row"), perm))

    nmsg = len(plan())
    vm = pl.BlockSpec(memory_space=pltpu.VMEM)
    G, U, V = pl.pallas_call(
        gather_factor,
        out_shape=(
            jax.ShapeDtypeStruct((2 * NC, 32, HALF), BF),
            jax.ShapeDtypeStruct((512, 512), F32),
            jax.ShapeDtypeStruct((4, 128, 128), F32),
        ),
        in_specs=[vm, vm],
        out_specs=(pl.BlockSpec(memory_space=pl.ANY), vm, vm),
        scratch_shapes=[
            pltpu.VMEM((512, 512), F32),
            pltpu.VMEM((4, 512, 128), BF),
            pltpu.SemaphoreType.DMA((2,)),
            pltpu.SemaphoreType.DMA((2,)),
            pltpu.SemaphoreType.DMA((nmsg,)),
            pltpu.SemaphoreType.DMA((1,)),
            pltpu.SemaphoreType.DMA((2,)),
            pltpu.SemaphoreType.DMA((4, 4)),
            pltpu.SemaphoreType.DMA((3, 4)),
        ],
        compiler_params=pltpu.CompilerParams(collective_id=0, has_side_effects=True),
        cost_estimate=pl.CostEstimate(flops=10**9, bytes_accessed=10**8, transcendentals=0),
        name="gather_factor",
    )(halves, pivot_block)

    mc = jnp.stack(pieces)
    tile = 768
    schur, pf, lf = pl.pallas_call(
        update,
        grid=(6144 // tile,),
        out_shape=(
            jax.ShapeDtypeStruct((6144, 128), BF),
            jax.ShapeDtypeStruct((32, 512), BF),
            jax.ShapeDtypeStruct((512, 128), F32),
        ),
        in_specs=[
            pl.BlockSpec((2, tile, HALF), lambda i: (0, i, 0)),
            pl.BlockSpec((tile, 128), lambda i: (i, 0)),
            pl.BlockSpec((4, 32, 512), lambda i: (0, 0, 0)),
            pl.BlockSpec((2, 32, HALF), lambda i: (0, 0, 0)),
            pl.BlockSpec((512, 512), lambda i: (0, 0)),
            pl.BlockSpec((4, 128, 128), lambda i: (0, 0, 0)),
        ],
        out_specs=(
            pl.BlockSpec((tile, 128), lambda i: (i, 0)),
            pl.BlockSpec((32, 512), lambda i: (0, 0)),
            pl.BlockSpec((512, 128), lambda i: (0, 0)),
        ),
        scratch_shapes=[pltpu.VMEM((256, 512), BF)],
        name="update",
    )(G.reshape(2, 6144, HALF), trailing, mc, halves, U, V)
    return lf, pf[None], schur


def solution(mesh):
    return jax.shard_map(
        body,
        mesh=mesh,
        in_specs=(P(None, "row"), P("row", "col", None), P("row", None), P("row", "col")),
        out_specs=(P(None, "row"), P("row", "col", None), P("row", "col")),
        check_vma=False,
    )
```

```python
import functools
import heapq

import jax
import jax.numpy as jnp
from jax import lax
from jax.experimental import pallas as pl
from jax.experimental.pallas import tpu as pltpu
from jax.sharding import PartitionSpec as P

F32 = jnp.float32
BF = jnp.bfloat16
MESH = pl.DeviceIdType.MESH
NZ, NY, NX, NR = 12, 8, 2, 4
NC = NZ * NY * NX
HALF = 256
POINTS = 16


def split(a):
    hi = a.astype(BF)
    return hi, (a - hi.astype(F32)).astype(BF)


def dot3(a, b, ca, cb):
    ah, al = split(a)
    bh, bl = split(b)
    d = functools.partial(
        lax.dot_general,
        dimension_numbers=(((ca,), (cb,)), ((), ())),
        preferred_element_type=F32,
    )
    return d(ah, bh) + (d(ah, bl) + d(al, bh))


def lane_b(x, j):
    return jnp.broadcast_to(x[:, j : j + 1], (8, 128))


def sub_b(x, i):
    return jnp.broadcast_to(x[i : i + 1, :], (8, 128))


def factor128(slabs, at):
    lane = lax.broadcasted_iota(jnp.int32, (8, 128), 1)
    sub = lax.broadcasted_iota(jnp.int32, (8, 128), 0)
    S = list(slabs)
    V = [jnp.where(lane == sub + 8 * p, F32(1.0), F32(0.0)) for p in range(16)]
    Us, Vs = [], []

    def gather_rows(rows):
        x = rows[0]
        for i in range(1, 8):
            x = jnp.where(sub == i, rows[i], x)
        return x

    for p in range(16):
        at(p)
        Sp, Vp = S[p], V[p]
        C = [lane_b(Sp, 8 * p + j) for j in range(8)]
        e = [[sub_b(C[j], i) for j in range(8)] for i in range(8)]
        r = [sub_b(Sp, i) for i in range(8)]
        v = [sub_b(Vp, i) for i in range(8)]
        d, ur, vr = [], [], []
        for j in range(8):
            inv = 1.0 / e[j][j]
            d.append(e[j][j])
            ur.append(r[j])
            vr.append(v[j])
            rj, vj = r[j] * inv, v[j] * inv
            ej = [e[j][m] * inv if m > j else None for m in range(8)]
            for i in range(8):
                if i != j:
                    f = e[i][j]
                    for m in range(j + 1, 8):
                        e[i][m] = e[i][m] - f * ej[m]
                    r[i] = r[i] - f * rj
                    v[i] = v[i] - f * vj
            r[j], v[j] = rj, vj
            for m in range(j + 1, 8):
                e[j][m] = ej[m]
        for q in range(p + 1, 16):
            T = [lane_b(S[q], 8 * p + j) for j in range(8)]
            a = [T[j] * r[j] for j in range(8)]
            b = [T[j] * v[j] for j in range(8)]
            while len(a) > 1:
                a = [a[i] + a[i + 1] for i in range(0, len(a), 2)]
                b = [b[i] + b[i + 1] for i in range(0, len(b), 2)]
            S[q] = S[q] - a[0]
            V[q] = V[q] - b[0]
        rs = lax.rsqrt(gather_rows(d))
        Us.append(jnp.where(lane >= sub + 8 * p, gather_rows(ur) * rs, F32(0.0)))
        Vs.append(gather_rows(vr) * rs)
    return Us, Vs


def reach(axis, sign, other):
    n = NZ if axis == "z" else NY
    return n // 2 if (other % 2 == 0) == (sign > 0) else n // 2 - 1


def plan():
    def children(half, dz, dy):
        last, first = ("y", "z") if half == 0 else ("z", "y")
        pos = {"z": dz, "y": dy}
        out = []

        def to(axis, new):
            q = dict(pos)
            q[axis] = new
            out.append((axis, new - pos[axis], (half, q["z"], q["y"])))

        if pos[last] == 0:
            here = pos[first]
            stage = 3 if first == "z" else 4
            if abs(here) % stage == 0:
                for sign in (1, -1):
                    if here == 0 or (here > 0) == (sign > 0):
                        for d in range(stage, 0, -1):
                            if abs(here) + d <= reach(first, sign, 0):
                                to(first, here + sign * d)
            for sign in (1, -1):
                to(last, sign)
        else:
            sign = 1 if pos[last] > 0 else -1
            if abs(pos[last]) + 1 <= reach(last, sign, pos[first]):
                to(last, pos[last] + sign)
        return out

    free = {}
    heap = [(3.0, 0, (0, 0, 0)), (3.0, 1, (1, 0, 0))]
    order = []
    count = 2
    wire = 0.71
    lag = {"z": 1.9, "y": 2.3}
    while heap:
        t, _, msg = heapq.heappop(heap)
        kids = children(*msg)
        order.append((t, msg, kids))
        for axis, delta, kid in kids:
            sign = 1 if delta > 0 else -1
            start = max(t, free.get((axis, sign), 0.0))
            free[(axis, sign)] = start + wire * abs(delta)
            done = start + wire + lag[axis] + 0.75 * (abs(delta) - 1)
            heapq.heappush(heap, (done, count, kid))
            count += 1
    return order


def gather_factor(
    x_ref, lead_ref, piv_ref, G, U, Z, PF, V, A, PV, MS, MC, sem_xs, sem_xr, sem_r, sem_s, sem_l, sem_p, sem_ps, sem_c, sem_cs
):
    col, row = lax.axis_index("col"), lax.axis_index("row")
    z, y, x = col // (NY * NX), (col // NX) % NY, col % NX

    def at_col(zz, yy, xx):
        return (zz * NY + yy) * NX + xx

    def wrap(v, n):
        return lax.rem(v + n, n)

    def away(axis, delta):
        return at_col(wrap(z + delta, NZ), y, x) if axis == "z" else at_col(z, wrap(y + delta, NY), x)

    def remote(src, dst, send, recv, c, r):
        return pltpu.make_async_remote_copy(
            src_ref=src, dst_ref=dst, send_sem=send, recv_sem=recv, device_id=(c, r), device_id_type=MESH
        )

    def wait(ref, sem):
        pltpu.make_async_copy(ref, ref, sem).wait()

    x_nbr = at_col(z, y, 1 - x)
    barrier = pltpu.get_barrier_semaphore()
    targets = [(x_nbr, row)]
    targets += [(away("z", d), row) for d in (-3, -2, -1, 1, 2, 3)]
    targets += [(away("y", d), row) for d in (-3, -2, -1, 1, 2, 3, 4)]
    targets += [(col, lax.rem(row + k, 4)) for k in range(1, 4)]
    for t in targets:
        pl.semaphore_signal(barrier, inc=1, device_id=t, device_id_type=MESH)

    lane = lax.broadcasted_iota(jnp.int32, (32, HALF), 1)
    first = lead_ref[0, col // 4]
    for half in range(2):
        kept = (lane + half * HALF) // 128 >= first
        MS[half] = jnp.where(kept, x_ref[0, :, half * HALF : half * HALF + HALF].astype(F32), 0.0).astype(BF)
    for i in range(4):

        @pl.when(row >= i)
        def _():
            pltpu.make_async_copy(
                piv_ref.at[pl.ds(128 * i, 128)], PV.at[row, pl.ds(128 * i, 128)], sem_p.at[row, i]
            ).start()

    pl.semaphore_wait(barrier, len(targets))

    own, xs = [], []
    for half in range(2):
        dst = G.at[pl.ds(half * NC + col, 1)]
        xs.append(remote(MS.at[pl.ds(half, 1)], dst, sem_xs.at[half], sem_xr.at[half], x_nbr, row))
        xs[half].start()
        own.append(pltpu.make_async_copy(MS.at[pl.ds(half, 1)], dst, sem_l.at[half]))
        own[half].start()

    for i in range(4):

        @pl.when(row >= i)
        def _():
            for k in range(1, 4):
                src, dst = piv_ref.at[pl.ds(128 * i, 128)], PV.at[row, pl.ds(128 * i, 128)]
                remote(src, dst, sem_ps.at[k - 1, i], sem_p.at[row, i], col, lax.rem(row + k, 4)).start()

    events = plan()
    index = {msg: i for i, (_, msg, _) in enumerate(events)}

    def pair(msg):
        half, dz, dy = msg
        zz, yy = wrap(z - dz, NZ), wrap(y - dy, NY)
        return G.at[pl.ds(half * NC + (zz * NY + yy) * NX, 2)]

    def handle(event):
        _, msg, kids = event
        half, dz, dy = msg
        ref = pair(msg)
        if dz == 0 and dy == 0:
            own[half].wait()
            xs[half].wait()
        else:
            wait(ref, sem_r.at[index[msg]])
        for axis, delta, kid in kids:
            remote(ref, ref, sem_s.at[0], sem_r.at[index[kid]], away(axis, delta), row).start()

    goal = 48 * row + col // 4
    here = lax.rem(col, 4)

    def far_send(_):
        for half in range(2):
            src, dst = MS.at[pl.ds(half, 1)], MC.at[pl.ds(4 * half + here, 1)]

            @pl.when(goal != col)
            def _():
                remote(src, dst, sem_cs.at[half], sem_c.at[4 * half + here], goal, row).start()

            @pl.when(goal == col)
            def _():
                pltpu.make_async_copy(src, dst, sem_c.at[4 * half + here]).start()

    root = col // 48

    def far_relay(_):
        @pl.when(row == root)
        def _():
            for i in range(8):
                wait(MC.at[pl.ds(i, 1)], sem_c.at[i])
            for k in range(1, 4):
                remote(MC, MC, sem_cs.at[1 + k], sem_c.at[8], col, lax.rem(row + k, 4)).start()

    def wait_piv(s, i):
        wait(PV.at[s, pl.ds(128 * i, 128)], sem_p.at[s, i])
        A[pl.ds(128 * i, 128), pl.ds(128 * s, 128)] = PV[s, pl.ds(128 * i, 128), :].astype(F32)

    near = max(t for t, (half, dz, dy), _ in events if half == 0 and dy == 0)
    todo = [(t, 0, functools.partial(handle, ev)) for ev in events for t in (ev[0],)]
    todo += [(near + 0.01, 1, functools.partial(far_send, None)), (near + 12.0, 2, functools.partial(far_relay, None))]
    todo.sort(key=lambda e: (e[0], e[1]))
    begin, block = 4.0, 7.0

    def run_until(t):
        while todo and todo[0][0] <= t:
            todo.pop(0)[2]()

    wait_piv(0, 0)
    for k in range(4):
        o = 128 * k

        def at(p):
            if p % (16 // POINTS) == 0:
                run_until(begin + block * (k + p / 16) - 0.3)

        D = A[o : o + 128, o : o + 128]
        Us, Vs = factor128([D[8 * p : 8 * p + 8] for p in range(16)], at)
        Vk = jnp.concatenate(Vs, axis=0)
        V[k] = Vk
        U[o : o + 128, o : o + 128] = jnp.concatenate(Us, axis=0)
        if k > 0:
            U[o : o + 128, 0:o] = jnp.zeros((128, o), F32)
        if k == 0:
            for s in range(1, 4):
                for i in range(s + 1):
                    wait_piv(s, i)
        if k < 3:
            rest = dot3(Vk, A[o : o + 128, o + 128 :], 1, 0)
            U[o : o + 128, o + 128 :] = rest
            for i in range(k + 1, 4):
                b = 128 * (i - k - 1)
                A[128 * i : 128 * i + 128, 128 * i :] -= dot3(rest[:, b : b + 128], rest[:, b:], 0, 0)

    run_until(begin + 4 * block)

    @pl.when(row != root)
    def _():
        wait(MC, sem_c.at[8])

    left = jnp.concatenate([MC[j] for j in range(4)] + [MS[0]], axis=0)
    right = jnp.concatenate([MC[4 + j] for j in range(4)] + [MS[1]], axis=0)
    rhs = [a[:, b : b + 128].astype(F32) for a in (left, right) for b in (0, 128)]
    for k in range(4):
        rhs[k] = dot3(rhs[k], V[k], 1, 1)
        for i in range(k + 1, 4):
            rhs[i] = rhs[i] - dot3(rhs[k], U[128 * k : 128 * k + 128, 128 * i : 128 * i + 128], 1, 0)
        PF[:, 128 * k : 128 * k + 128] = rhs[k][128:160].astype(BF)
        run_until(begin + 4 * block + 0.7 * (k + 1))
    back = [a[:128] for a in rhs]
    for k in range(3, -1, -1):
        zk = dot3(back[k], V[k], 1, 0)
        hi, lo = split(zk)
        Z[0:128, 128 * k : 128 * k + 128] = hi
        Z[128:256, 128 * k : 128 * k + 128] = lo
        for i in range(k):
            back[i] = back[i] - dot3(zk, U[128 * i : 128 * i + 128, 128 * k : 128 * k + 128], 1, 1)
        run_until(begin + 4 * block + 0.7 * (8 - k))
    run_until(1e9)

    sent = sum(len(kids) for _, _, kids in events)
    wait(G.at[pl.ds(0, 2 * sent)], sem_s.at[0])
    for i in range(4):

        @pl.when(row >= i)
        def _():
            for k in range(1, 4):
                wait(piv_ref.at[pl.ds(128 * i, 128)], sem_ps.at[k - 1, i])

    @pl.when(goal != col)
    def _():
        for half in range(2):
            wait(MS.at[pl.ds(half, 1)], sem_cs.at[half])

    @pl.when(row == root)
    def _():
        for k in range(1, 4):
            wait(MC, sem_cs.at[1 + k])


def update(g_ref, t_ref, z_ref, pf_ref, u_ref, s_ref, p_ref, l_ref):
    @pl.when(pl.program_id(0) == 0)
    def _():
        p_ref[0] = pf_ref[...]
        o = pl.multiple_of(lax.axis_index("row") * 128, 128)
        l_ref[...] = u_ref[pl.ds(o, 128), :].T

    dims = (((1,), (1,)), ((), ()))
    acc = lax.dot_general(g_ref[0], z_ref[:, 0:HALF], dims, preferred_element_type=F32)
    acc = acc + lax.dot_general(g_ref[1], z_ref[:, HALF:], dims, preferred_element_type=F32)
    s_ref[...] = (t_ref[...].astype(F32) - (acc[:, 0:128] + acc[:, 128:256])).astype(BF)


def body(pivot_block, panel, lead, trailing):
    nmsg = len(plan())
    vm = pl.BlockSpec(memory_space=pltpu.VMEM)
    dma = pltpu.SemaphoreType.DMA
    G, U, Z, PF = pl.pallas_call(
        gather_factor,
        out_shape=(
            jax.ShapeDtypeStruct((2 * NC, 32, HALF), BF),
            jax.ShapeDtypeStruct((512, 512), F32),
            jax.ShapeDtypeStruct((256, 512), BF),
            jax.ShapeDtypeStruct((32, 512), BF),
        ),
        in_specs=[vm, pl.BlockSpec(memory_space=pltpu.SMEM), vm],
        out_specs=(pl.BlockSpec(memory_space=pl.ANY), vm, vm, vm),
        scratch_shapes=[
            pltpu.VMEM((4, 128, 128), F32),
            pltpu.VMEM((512, 512), F32),
            pltpu.VMEM((4, 512, 128), BF),
            pltpu.VMEM((2, 32, HALF), BF),
            pltpu.VMEM((8, 32, HALF), BF),
            dma((2,)),
            dma((2,)),
            dma((nmsg,)),
            dma((1,)),
            dma((2,)),
            dma((4, 4)),
            dma((3, 4)),
            dma((9,)),
            dma((5,)),
        ],
        compiler_params=pltpu.CompilerParams(collective_id=0, has_side_effects=True),
        name="gather_factor",
    )(panel, lead, pivot_block)

    tile = 768
    schur, pf, lf = pl.pallas_call(
        update,
        grid=(6144 // tile,),
        out_shape=(
            jax.ShapeDtypeStruct((6144, 128), BF),
            jax.ShapeDtypeStruct((1, 32, 512), BF),
            jax.ShapeDtypeStruct((512, 128), F32),
        ),
        in_specs=[
            pl.BlockSpec((2, tile, HALF), lambda i: (0, i, 0)),
            pl.BlockSpec((tile, 128), lambda i: (i, 0)),
            pl.BlockSpec((256, 512), lambda i: (0, 0)),
            pl.BlockSpec((32, 512), lambda i: (0, 0)),
            pl.BlockSpec((512, 512), lambda i: (0, 0)),
        ],
        out_specs=(
            pl.BlockSpec((tile, 128), lambda i: (i, 0)),
            pl.BlockSpec((1, 32, 512), lambda i: (0, 0, 0)),
            pl.BlockSpec((512, 128), lambda i: (0, 0)),
        ),
        name="update",
    )(G.reshape(2, 6144, HALF), trailing, Z, PF, U)
    return lf, pf, schur


def solution(mesh):
    return jax.shard_map(
        body,
        mesh=mesh,
        in_specs=(P(None, "row"), P("row", "col", None), P("row", None), P("row", "col")),
        out_specs=(P(None, "row"), P("row", "col", None), P("row", "col")),
        check_vma=False,
    )
```

```python
import functools
import heapq

import jax
import jax.numpy as jnp
from jax import lax
from jax.experimental import pallas as pl
from jax.experimental.pallas import tpu as pltpu
from jax.sharding import PartitionSpec as P

F32 = jnp.float32
BF = jnp.bfloat16
MESH = pl.DeviceIdType.MESH
NZ, NY, NX, NR = 12, 8, 2, 4
NC = NZ * NY * NX
HALF = 256
POINTS = 16


def split(a):
    hi = a.astype(BF)
    return hi, (a - hi.astype(F32)).astype(BF)


def dot3(a, b, ca, cb):
    ah, al = split(a)
    bh, bl = split(b)
    d = functools.partial(
        lax.dot_general,
        dimension_numbers=(((ca,), (cb,)), ((), ())),
        preferred_element_type=F32,
    )
    return d(ah, bh) + (d(ah, bl) + d(al, bh))


def lane_b(x, j):
    return jnp.broadcast_to(x[:, j : j + 1], (8, 128))


def sub_b(x, i):
    return jnp.broadcast_to(x[i : i + 1, :], (8, 128))


def factor128(slabs, at):
    lane = lax.broadcasted_iota(jnp.int32, (8, 128), 1)
    sub = lax.broadcasted_iota(jnp.int32, (8, 128), 0)
    S = list(slabs)
    V = [jnp.where(lane == sub + 8 * p, F32(1.0), F32(0.0)) for p in range(16)]
    Us, Vs = [], []

    def gather_rows(rows):
        x = rows[0]
        for i in range(1, 8):
            x = jnp.where(sub == i, rows[i], x)
        return x

    for p in range(16):
        at(p)
        Sp, Vp = S[p], V[p]
        C = [lane_b(Sp, 8 * p + j) for j in range(8)]
        e = [[sub_b(C[j], i) for j in range(8)] for i in range(8)]
        r = [sub_b(Sp, i) for i in range(8)]
        v = [sub_b(Vp, i) for i in range(8)]
        d, ur, vr = [], [], []
        for j in range(8):
            inv = 1.0 / e[j][j]
            d.append(e[j][j])
            ur.append(r[j])
            vr.append(v[j])
            rj, vj = r[j] * inv, v[j] * inv
            ej = [e[j][m] * inv if m > j else None for m in range(8)]
            for i in range(8):
                if i != j:
                    f = e[i][j]
                    for m in range(j + 1, 8):
                        e[i][m] = e[i][m] - f * ej[m]
                    r[i] = r[i] - f * rj
                    v[i] = v[i] - f * vj
            r[j], v[j] = rj, vj
            for m in range(j + 1, 8):
                e[j][m] = ej[m]
        for q in range(p + 1, 16):
            T = [lane_b(S[q], 8 * p + j) for j in range(8)]
            a = [T[j] * r[j] for j in range(8)]
            b = [T[j] * v[j] for j in range(8)]
            while len(a) > 1:
                a = [a[i] + a[i + 1] for i in range(0, len(a), 2)]
                b = [b[i] + b[i + 1] for i in range(0, len(b), 2)]
            S[q] = S[q] - a[0]
            V[q] = V[q] - b[0]
        rs = lax.rsqrt(gather_rows(d))
        Us.append(jnp.where(lane >= sub + 8 * p, gather_rows(ur) * rs, F32(0.0)))
        Vs.append(gather_rows(vr) * rs)
    return Us, Vs


def reach(axis, sign, other):
    n = NZ if axis == "z" else NY
    return n // 2 if (other % 2 == 0) == (sign > 0) else n // 2 - 1


def plan():
    stages = {"z": 2, "y": 4}
    lag = {"z": 2.3, "y": 2.8, "x": 2.5}
    wire = 0.71

    def kind(half, dz, dy):
        far, side = (dy, dz) if half == 0 else (dz, dy)
        return "s" if far != 0 and abs(side) < 2 else "p"

    def children(half, dz, dy, k):
        if k == "x":
            return []
        last, first = ("y", "z") if half == 0 else ("z", "y")
        pos = {"z": dz, "y": dy}
        out = []

        def to(axis, new):
            q = dict(pos)
            q[axis] = new
            out.append((axis, new - pos[axis], (half, q["z"], q["y"], kind(half, q["z"], q["y"]))))

        if pos[last] == 0:
            here = pos[first]
            if here != 0 and abs(here) % stages[first] == 0:
                sign = 1 if here > 0 else -1
                for d in range(stages[first], 0, -1):
                    if abs(here) + d <= reach(first, sign, 0):
                        to(first, here + sign * d)
            for sign in (1, -1):
                to(last, sign)
        else:
            sign = 1 if pos[last] > 0 else -1
            if abs(pos[last]) + 1 <= reach(last, sign, pos[first]):
                to(last, pos[last] + sign)
        if k == "s":
            out.append(("x", 0, (half, dz, dy, "x")))
        return out

    free = {}
    heap = []
    order = []
    start = []
    count = 0

    def send(t, axis, delta, kid):
        nonlocal count
        w = wire if kid[3] == "p" else wire / 2
        key = (axis, delta > 0)
        begin = max(t, free.get(key, 0.0))
        free[key] = begin + w * max(1, abs(delta))
        heapq.heappush(heap, (begin + w + lag[axis] + 0.75 * max(0, abs(delta) - 1), count, kid))
        count += 1

    for d in range(4, 0, -1):
        for half, axis in ((0, "z"), (1, "y")):
            for sign in (1, -1):
                if d <= stages[axis] and d <= reach(axis, sign, 0):
                    kid = (0, sign * d, 0, "p") if axis == "z" else (1, 0, sign * d, "p")
                    start.append((axis, sign * d, kid))
                    send(0.0, axis, sign * d, kid)
    for half in range(2):
        heapq.heappush(heap, (3.0, count, (half, 0, 0, "p")))
        count += 1
    while heap:
        t, _, msg = heapq.heappop(heap)
        kids = children(*msg)
        order.append((t, msg, kids))
        for axis, delta, kid in kids:
            send(t, axis, delta, kid)
    return start, order


def step(
    x_ref, lead_ref, piv_ref, t_ref, s_ref, p_ref, l_ref,
    G, T, ACC, OUT, U, Z, V, A, PV, MS, MC,
    sem_xs, sem_xr, sem_r, sem_s, sem_l, sem_p, sem_ps, sem_c, sem_cs, sem_t,
):
    col, row = lax.axis_index("col"), lax.axis_index("row")
    z, y, x = col // (NY * NX), (col // NX) % NY, col % NX

    def wrap(v, n):
        return lax.rem(v + n, n)

    def away(axis, delta, xx):
        if axis == "x":
            return (z * NY + y) * NX + 1 - x
        if axis == "z":
            return (wrap(z + delta, NZ) * NY + y) * NX + xx
        return (z * NY + wrap(y + delta, NY)) * NX + xx

    def remote(src, dst, send, recv, c, r):
        return pltpu.make_async_remote_copy(
            src_ref=src, dst_ref=dst, send_sem=send, recv_sem=recv, device_id=(c, r), device_id_type=MESH
        )

    def wait(ref, sem):
        pltpu.make_async_copy(ref, ref, sem).wait()

    start, events = plan()
    barrier = pltpu.get_barrier_semaphore()
    targets = [(away("x", 0, x), row)]
    for xx in (x, 1 - x):
        targets += [(away("z", d, xx), row) for d in (-2, -1, 1, 2)]
        targets += [(away("y", d, xx), row) for d in (-3, -2, -1, 1, 2, 3, 4)]
    targets += [(col, lax.rem(row + k, 4)) for k in range(1, 4)]
    for t in targets:
        pl.semaphore_signal(barrier, inc=1, device_id=t, device_id_type=MESH)

    fetch = pltpu.make_async_copy(t_ref, T, sem_t.at[0])
    fetch.start()
    lane = lax.broadcasted_iota(jnp.int32, (32, HALF), 1)
    first = lead_ref[0, col // 4]
    for half in range(2):
        kept = (lane + half * HALF) // 128 >= first
        MS[half] = jnp.where(kept, x_ref[0, :, half * HALF : half * HALF + HALF].astype(F32), 0.0).astype(BF)
    for i in range(4):

        @pl.when(row >= i)
        def _():
            pltpu.make_async_copy(
                piv_ref.at[pl.ds(128 * i, 128)], PV.at[row, pl.ds(128 * i, 128)], sem_p.at[row, i]
            ).start()

    pl.semaphore_wait(barrier, len(targets))

    def send_piv(i):
        @pl.when(row >= i)
        def _():
            for k in range(1, 4):
                src, dst = piv_ref.at[pl.ds(128 * i, 128)], PV.at[row, pl.ds(128 * i, 128)]
                remote(src, dst, sem_ps.at[k - 1, i], sem_p.at[row, i], col, lax.rem(row + k, 4)).start()

    own, xs = [], []
    for half in range(2):
        dst = G.at[pl.ds(half * NC + col, 1)]
        xs.append(remote(MS.at[pl.ds(half, 1)], dst, sem_xs.at[half], sem_xr.at[half], away("x", 0, x), row))
        xs[half].start()
        own.append(pltpu.make_async_copy(MS.at[pl.ds(half, 1)], dst, sem_l.at[half]))
        own[half].start()
    send_piv(0)

    index = {msg: i for i, (_, msg, _) in enumerate(events)}
    both = {kid: i for i, (_, _, kid) in enumerate(start)}
    sent = [0]

    def send_sem(n):
        if sent[-1] + n > 2 * NC:
            sent.append(0)
        sent[-1] += n
        return sem_s.at[len(sent) - 1]

    for axis, delta, kid in start:
        src, dst = MS.at[pl.ds(kid[0], 1)], G.at[pl.ds(kid[0] * NC + col, 1)]
        for xx in (x, 1 - x):
            remote(src, dst, send_sem(1), sem_r.at[len(events) + 2 * both[kid] + x], away(axis, delta, xx), row).start()
    for i in range(1, 4):
        send_piv(i)

    def part(half, dz, dy, k):
        base = half * NC + (wrap(z - dz, NZ) * NY + wrap(y - dy, NY)) * NX
        if k == "p":
            return G.at[pl.ds(base, 2)]
        return G.at[pl.ds(base + (x if k == "s" else 1 - x), 1)]

    def handle(event):
        _, msg, kids = event
        half, dz, dy, k = msg
        ref = part(*msg)
        if dz == 0 and dy == 0:
            own[half].wait()
            xs[half].wait()
        elif msg in both:
            for q in range(2):
                wait(ref.at[pl.ds(q, 1)], sem_r.at[len(events) + 2 * both[msg] + q])
        else:
            wait(ref, sem_r.at[index[msg]])
        for axis, delta, kid in kids:
            pairs = k == "p" and kid[3] == "p"
            src = ref if pairs or k == "s" else part(half, dz, dy, "s")
            remote(src, src, send_sem(2 if pairs else 1), sem_r.at[index[kid]], away(axis, delta, x), row).start()

    goal = 48 * row + col // 4
    here = lax.rem(col, 4)

    def far_send():
        for half in range(2):
            src, dst = MS.at[pl.ds(half, 1)], MC.at[pl.ds(4 * half + here, 1)]

            @pl.when(goal != col)
            def _():
                remote(src, dst, sem_cs.at[half], sem_c.at[4 * half + here], goal, row).start()

            @pl.when(goal == col)
            def _():
                pltpu.make_async_copy(src, dst, sem_c.at[4 * half + here]).start()

    root = col // 48

    def far_relay():
        @pl.when(row == root)
        def _():
            for i in range(8):
                wait(MC.at[pl.ds(i, 1)], sem_c.at[i])
            for k in range(1, 4):
                remote(MC, MC, sem_cs.at[1 + k], sem_c.at[8], col, lax.rem(row + k, 4)).start()

    def wait_piv(s, i):
        wait(PV.at[s, pl.ds(128 * i, 128)], sem_p.at[s, i])
        A[pl.ds(128 * i, 128), pl.ds(128 * s, 128)] = PV[s, pl.ds(128 * i, 128), :].astype(F32)

    def widen():
        fetch.wait()

        @pl.loop(0, 12)
        def _(i):
            ACC[pl.ds(16 * i, 16)] = T[pl.ds(16 * i, 16)].astype(F32)

    dims = (((1,), (1,)), ((), ()))

    def product(m, half):
        acc = lax.dot_general(m, Z[:, half * HALF : half * HALF + HALF], dims, preferred_element_type=F32)
        return acc[:, 0:128] + acc[:, 128:256]

    def plane_y(dy):
        yy = wrap(y - dy, NY)
        at = [pl.ds((zz * NY + yy) * NX, 2) for zz in range(NZ)]
        m = jnp.concatenate([G[a] for a in at], axis=0).reshape(NZ * 64, HALF)
        d = product(m, 0).reshape(NZ * 2, 32, 128)
        for zz in range(NZ):
            ACC[at[zz]] -= d[2 * zz : 2 * zz + 2]

    def plane_z(dz):
        b = wrap(z - dz, NZ) * (NY * NX)
        m = G[pl.ds(NC + b, 16)].reshape(512, HALF)
        ACC[pl.ds(b, 16)] -= product(m, 1).reshape(16, 32, 128)

    near = max(t for t, (half, dz, dy, _), _ in events if half == 0 and dy == 0)
    todo = [(ev[0], 0, functools.partial(handle, ev)) for ev in events]
    todo += [(near + 0.01, 1, far_send), (near + 1.0, 2, widen), (near + 12.0, 3, far_relay)]
    begin, block = 4.0, 7.0
    solved = begin + 4 * block + 5.5
    planes = []
    for half, n, f in ((0, NY, plane_y), (1, NZ, plane_z)):
        for d in range(n):
            ready = max(ev[0] for ev in events if ev[1][0] == half and (ev[1][2 - half] - d) % n == 0)
            planes.append((ready, functools.partial(f, d)))
    planes.sort(key=lambda e: e[0])
    for i, (ready, f) in enumerate(planes):
        todo.append((max(ready + 0.01, solved + 0.4 * i), 4, f))
    todo.sort(key=lambda e: (e[0], e[1]))

    def run_until(t):
        while todo and todo[0][0] <= t:
            todo.pop(0)[2]()

    wait_piv(0, 0)
    for k in range(4):
        o = 128 * k

        def at(p):
            if p % (16 // POINTS) == 0:
                run_until(begin + block * (k + p / 16) - 0.3)

        D = A[o : o + 128, o : o + 128]
        Us, Vs = factor128([D[8 * p : 8 * p + 8] for p in range(16)], at)
        Vk = jnp.concatenate(Vs, axis=0)
        V[k] = Vk
        U[o : o + 128, o : o + 128] = jnp.concatenate(Us, axis=0)
        if k > 0:
            U[o : o + 128, 0:o] = jnp.zeros((128, o), F32)
        if k == 0:
            for s in range(1, 4):
                for i in range(s + 1):
                    wait_piv(s, i)
        if k < 3:
            rest = dot3(Vk, A[o : o + 128, o + 128 :], 1, 0)
            U[o : o + 128, o + 128 :] = rest
            for i in range(k + 1, 4):
                b = 128 * (i - k - 1)
                A[128 * i : 128 * i + 128, 128 * i :] -= dot3(rest[:, b : b + 128], rest[:, b:], 0, 0)

    run_until(begin + 4 * block)

    @pl.when(row != root)
    def _():
        wait(MC, sem_c.at[8])

    left = jnp.concatenate([MC[j] for j in range(4)] + [MS[0]], axis=0)
    right = jnp.concatenate([MC[4 + j] for j in range(4)] + [MS[1]], axis=0)
    rhs = [a[:, b : b + 128].astype(F32) for a in (left, right) for b in (0, 128)]
    for k in range(4):
        rhs[k] = dot3(rhs[k], V[k], 1, 1)
        for i in range(k + 1, 4):
            rhs[i] = rhs[i] - dot3(rhs[k], U[128 * k : 128 * k + 128, 128 * i : 128 * i + 128], 1, 0)
        p_ref[0, :, 128 * k : 128 * k + 128] = rhs[k][128:160].astype(BF)
        run_until(begin + 4 * block + 0.7 * (k + 1))
    back = [a[:128] for a in rhs]
    for k in range(3, -1, -1):
        zk = dot3(back[k], V[k], 1, 0)
        hi, lo = split(zk)
        Z[0:128, 128 * k : 128 * k + 128] = hi
        Z[128:256, 128 * k : 128 * k + 128] = lo
        for i in range(k):
            back[i] = back[i] - dot3(zk, U[128 * i : 128 * i + 128, 128 * k : 128 * k + 128], 1, 1)
        run_until(min(solved - 0.1, begin + 4 * block + 0.7 * (8 - k)))
    run_until(solved + 0.1)
    l_ref[...] = U[pl.ds(pl.multiple_of(row * 128, 128), 128), :].T
    run_until(1e9)

    outs = []
    for i in range(4):
        a = pl.ds(48 * i, 48)
        OUT[a] = ACC[a].astype(BF)
        outs.append(pltpu.make_async_copy(OUT.at[a], s_ref.at[a], sem_t.at[1 + i]))
        outs[i].start()

    for i, n in enumerate(sent):
        wait(G.at[pl.ds(0, n)], sem_s.at[i])
    for i in range(4):

        @pl.when(row >= i)
        def _():
            for k in range(1, 4):
                wait(piv_ref.at[pl.ds(128 * i, 128)], sem_ps.at[k - 1, i])

    @pl.when(goal != col)
    def _():
        for half in range(2):
            wait(MS.at[pl.ds(half, 1)], sem_cs.at[half])

    @pl.when(row == root)
    def _():
        for k in range(1, 4):
            wait(MC, sem_cs.at[1 + k])

    for c in outs:
        c.wait()


def body(pivot_block, panel, lead, trailing):
    start, events = plan()
    vm = pl.BlockSpec(memory_space=pltpu.VMEM)
    hbm = pl.BlockSpec(memory_space=pl.ANY)
    dma = pltpu.SemaphoreType.DMA
    schur, pf, lf = pl.pallas_call(
        step,
        out_shape=(
            jax.ShapeDtypeStruct((NC, 32, 128), BF),
            jax.ShapeDtypeStruct((1, 32, 512), BF),
            jax.ShapeDtypeStruct((512, 128), F32),
        ),
        in_specs=[vm, pl.BlockSpec(memory_space=pltpu.SMEM), vm, hbm],
        out_specs=(hbm, vm, vm),
        scratch_shapes=[
            pltpu.VMEM((2 * NC, 32, HALF), BF),
            pltpu.VMEM((NC, 32, 128), BF),
            pltpu.VMEM((NC, 32, 128), F32),
            pltpu.VMEM((NC, 32, 128), BF),
            pltpu.VMEM((512, 512), F32),
            pltpu.VMEM((256, 512), BF),
            pltpu.VMEM((4, 128, 128), F32),
            pltpu.VMEM((512, 512), F32),
            pltpu.VMEM((4, 512, 128), BF),
            pltpu.VMEM((2, 32, HALF), BF),
            pltpu.VMEM((8, 32, HALF), BF),
            dma((2,)),
            dma((2,)),
            dma((len(events) + 2 * len(start),)),
            dma((2,)),
            dma((2,)),
            dma((4, 4)),
            dma((3, 4)),
            dma((9,)),
            dma((5,)),
            dma((5,)),
        ],
        compiler_params=pltpu.CompilerParams(collective_id=0, has_side_effects=True, vmem_limit_bytes=48 * 2**20),
        name="cholesky_step",
    )(panel, lead, pivot_block, trailing.reshape(NC, 32, 128))
    return lf, pf, schur.reshape(6144, 128)


def solution(mesh):
    return jax.shard_map(
        body,
        mesh=mesh,
        in_specs=(P(None, "row"), P("row", "col", None), P("row", None), P("row", "col")),
        out_specs=(P(None, "row"), P("row", "col", None), P("row", "col")),
        check_vma=False,
    )
```

```python
import functools
import heapq

import jax
import jax.numpy as jnp
from jax import lax
from jax.experimental import pallas as pl
from jax.experimental.pallas import tpu as pltpu
from jax.sharding import PartitionSpec as P

F32 = jnp.float32
BF = jnp.bfloat16
MESH = pl.DeviceIdType.MESH
NZ, NY, NX, NR = 12, 8, 2, 4
NC = NZ * NY * NX
HALF = 256
POINTS = 16


def split(a):
    hi = a.astype(BF)
    return hi, (a - hi.astype(F32)).astype(BF)


def dot3(a, b, ca, cb):
    ah, al = split(a)
    bh, bl = split(b)
    d = functools.partial(
        lax.dot_general,
        dimension_numbers=(((ca,), (cb,)), ((), ())),
        preferred_element_type=F32,
    )
    return d(ah, bh) + (d(ah, bl) + d(al, bh))


def lane_b(x, j):
    return jnp.broadcast_to(x[:, j : j + 1], (8, 128))


def sub_b(x, i):
    return jnp.broadcast_to(x[i : i + 1, :], (8, 128))


def factor128(slabs, at):
    lane = lax.broadcasted_iota(jnp.int32, (8, 128), 1)
    sub = lax.broadcasted_iota(jnp.int32, (8, 128), 0)
    S = list(slabs)
    V = [jnp.where(lane == sub + 8 * p, F32(1.0), F32(0.0)) for p in range(16)]
    Us, Vs = [], []

    def gather_rows(rows):
        x = rows[0]
        for i in range(1, 8):
            x = jnp.where(sub == i, rows[i], x)
        return x

    for p in range(16):
        at(p)
        Sp, Vp = S[p], V[p]
        C = [lane_b(Sp, 8 * p + j) for j in range(8)]
        e = [[sub_b(C[j], i) for j in range(8)] for i in range(8)]
        r = [sub_b(Sp, i) for i in range(8)]
        v = [sub_b(Vp, i) for i in range(8)]
        d, ur, vr = [], [], []
        for j in range(8):
            inv = 1.0 / e[j][j]
            d.append(e[j][j])
            ur.append(r[j])
            vr.append(v[j])
            rj, vj = r[j] * inv, v[j] * inv
            ej = [e[j][m] * inv if m > j else None for m in range(8)]
            for i in range(8):
                if i != j:
                    f = e[i][j]
                    for m in range(j + 1, 8):
                        e[i][m] = e[i][m] - f * ej[m]
                    r[i] = r[i] - f * rj
                    v[i] = v[i] - f * vj
            r[j], v[j] = rj, vj
            for m in range(j + 1, 8):
                e[j][m] = ej[m]
        for q in range(p + 1, 16):
            T = [lane_b(S[q], 8 * p + j) for j in range(8)]
            a = [T[j] * r[j] for j in range(8)]
            b = [T[j] * v[j] for j in range(8)]
            while len(a) > 1:
                a = [a[i] + a[i + 1] for i in range(0, len(a), 2)]
                b = [b[i] + b[i + 1] for i in range(0, len(b), 2)]
            S[q] = S[q] - a[0]
            V[q] = V[q] - b[0]
        rs = lax.rsqrt(gather_rows(d))
        Us.append(jnp.where(lane >= sub + 8 * p, gather_rows(ur) * rs, F32(0.0)))
        Vs.append(gather_rows(vr) * rs)
    return Us, Vs


def reach(axis, sign, other):
    n = NZ if axis == "z" else NY
    return n // 2 if (other % 2 == 0) == (sign > 0) else n // 2 - 1


def plan():
    stages = {"z": 2, "y": 4}
    lag = {"z": 2.8, "y": 3.5, "x": 3.5}
    wire = 0.71

    def kind(half, dz, dy):
        far, side = (dy, dz) if half == 0 else (dz, dy)
        return "s" if far != 0 and abs(side) < (3 if half == 0 else 2) else "p"

    def children(half, dz, dy, k):
        if k == "x":
            return []
        last, first = ("y", "z") if half == 0 else ("z", "y")
        pos = {"z": dz, "y": dy}
        out = []

        def to(axis, new):
            q = dict(pos)
            q[axis] = new
            out.append((axis, new - pos[axis], (half, q["z"], q["y"], kind(half, q["z"], q["y"]))))

        if pos[last] == 0:
            here = pos[first]
            if here != 0 and abs(here) % stages[first] == 0:
                sign = 1 if here > 0 else -1
                for d in range(stages[first], 0, -1):
                    if abs(here) + d <= reach(first, sign, 0):
                        to(first, here + sign * d)
            for sign in (1, -1):
                to(last, sign)
        else:
            sign = 1 if pos[last] > 0 else -1
            if abs(pos[last]) + 1 <= reach(last, sign, pos[first]):
                to(last, pos[last] + sign)
        if k == "s":
            out.append(("x", 0, (half, dz, dy, "x")))
        return out

    free = {}
    heap = []
    order = []
    start = []
    count = 0

    def send(t, axis, delta, kid):
        nonlocal count
        w = wire if kid[3] == "p" else wire / 2
        key = (axis, delta > 0)
        begin = max(t, free.get(key, 0.0))
        free[key] = begin + w * max(1, abs(delta))
        heapq.heappush(heap, (begin + w + lag[axis] + 0.75 * max(0, abs(delta) - 1), count, kid))
        count += 1

    for d in range(4, 0, -1):
        for half, axis in ((0, "z"), (1, "y")):
            for sign in (1, -1):
                if d <= stages[axis] and d <= reach(axis, sign, 0):
                    kid = (0, sign * d, 0, "p") if axis == "z" else (1, 0, sign * d, "p")
                    start.append((axis, sign * d, kid))
                    send(0.0, axis, sign * d, kid)
    for half in range(2):
        heapq.heappush(heap, (4.0, count, (half, 0, 0, "p")))
        count += 1
    while heap:
        t, _, msg = heapq.heappop(heap)
        kids = children(*msg)
        order.append((t, msg, kids))
        for axis, delta, kid in kids:
            send(t, axis, delta, kid)
    return start, order


def step(
    x_ref, lead_ref, piv_ref, t_ref, s_ref, p_ref, l_ref,
    G, T, ACC, OUT, U, Z, V, A, PV, MS, MC,
    sem_xs, sem_xr, sem_r, sem_s, sem_l, sem_p, sem_ps, sem_c, sem_cs, sem_t,
):
    col, row = lax.axis_index("col"), lax.axis_index("row")
    z, y, x = col // (NY * NX), (col // NX) % NY, col % NX

    def wrap(v, n):
        return lax.rem(v + n, n)

    def away(axis, delta, xx):
        if axis == "x":
            return (z * NY + y) * NX + 1 - x
        if axis == "z":
            return (wrap(z + delta, NZ) * NY + y) * NX + xx
        return (z * NY + wrap(y + delta, NY)) * NX + xx

    def remote(src, dst, send, recv, c, r):
        return pltpu.make_async_remote_copy(
            src_ref=src, dst_ref=dst, send_sem=send, recv_sem=recv, device_id=(c, r), device_id_type=MESH
        )

    def wait(ref, sem):
        pltpu.make_async_copy(ref, ref, sem).wait()

    start, events = plan()
    barrier = pltpu.get_barrier_semaphore()
    targets = [(away("x", 0, x), row)]
    for xx in (x, 1 - x):
        targets += [(away("z", d, xx), row) for d in (-2, -1, 1, 2)]
        targets += [(away("y", d, xx), row) for d in (-3, -2, -1, 1, 2, 3, 4)]
    targets += [(col, lax.rem(row + k, 4)) for k in range(1, 4)]
    for t in targets:
        pl.semaphore_signal(barrier, inc=1, device_id=t, device_id_type=MESH)

    fetch = pltpu.make_async_copy(t_ref, T, sem_t.at[0])
    fetch.start()
    lane = lax.broadcasted_iota(jnp.int32, (32, HALF), 1)
    first = lead_ref[0, col // 4]
    for half in range(2):
        kept = (lane + half * HALF) // 128 >= first
        MS[half] = jnp.where(kept, x_ref[0, :, half * HALF : half * HALF + HALF].astype(F32), 0.0).astype(BF)
    for i in range(4):

        @pl.when(row >= i)
        def _():
            pltpu.make_async_copy(
                piv_ref.at[pl.ds(128 * i, 128)], PV.at[row, pl.ds(128 * i, 128)], sem_p.at[row, i]
            ).start()

    pl.semaphore_wait(barrier, len(targets))

    def send_piv(i):
        @pl.when(row >= i)
        def _():
            for k in range(1, 4):
                src, dst = piv_ref.at[pl.ds(128 * i, 128)], PV.at[row, pl.ds(128 * i, 128)]
                remote(src, dst, sem_ps.at[k - 1, i], sem_p.at[row, i], col, lax.rem(row + k, 4)).start()

    own, xs = [], []
    for half in range(2):
        dst = G.at[pl.ds(half * NC + col, 1)]
        xs.append(remote(MS.at[pl.ds(half, 1)], dst, sem_xs.at[half], sem_xr.at[half], away("x", 0, x), row))
        xs[half].start()
        own.append(pltpu.make_async_copy(MS.at[pl.ds(half, 1)], dst, sem_l.at[half]))
        own[half].start()
    send_piv(0)

    index = {msg: i for i, (_, msg, _) in enumerate(events)}
    both = {kid: i for i, (_, _, kid) in enumerate(start)}
    sent = [0]

    def send_sem(n):
        if sent[-1] + n > 2 * NC:
            sent.append(0)
        sent[-1] += n
        return sem_s.at[len(sent) - 1]

    for axis, delta, kid in start:
        src, dst = MS.at[pl.ds(kid[0], 1)], G.at[pl.ds(kid[0] * NC + col, 1)]
        for xx in (x, 1 - x):
            remote(src, dst, send_sem(1), sem_r.at[len(events) + 2 * both[kid] + x], away(axis, delta, xx), row).start()
    for i in range(1, 4):
        send_piv(i)

    def part(half, dz, dy, k):
        base = half * NC + (wrap(z - dz, NZ) * NY + wrap(y - dy, NY)) * NX
        if k == "p":
            return G.at[pl.ds(base, 2)]
        return G.at[pl.ds(base + (x if k == "s" else 1 - x), 1)]

    def handle(event):
        _, msg, kids = event
        half, dz, dy, k = msg
        ref = part(*msg)
        if dz == 0 and dy == 0:
            own[half].wait()
            xs[half].wait()
        elif msg in both:
            for q in range(2):
                wait(ref.at[pl.ds(q, 1)], sem_r.at[len(events) + 2 * both[msg] + q])
        else:
            wait(ref, sem_r.at[index[msg]])
        for axis, delta, kid in kids:
            pairs = k == "p" and kid[3] == "p"
            src = ref if pairs or k == "s" else part(half, dz, dy, "s")
            remote(src, src, send_sem(2 if pairs else 1), sem_r.at[index[kid]], away(axis, delta, x), row).start()

    goal = 48 * row + col // 4
    here = lax.rem(col, 4)

    def far_send():
        for half in range(2):
            src, dst = MS.at[pl.ds(half, 1)], MC.at[pl.ds(4 * half + here, 1)]

            @pl.when(goal != col)
            def _():
                remote(src, dst, sem_cs.at[half], sem_c.at[4 * half + here], goal, row).start()

            @pl.when(goal == col)
            def _():
                pltpu.make_async_copy(src, dst, sem_c.at[4 * half + here]).start()

    root = col // 48

    def far_relay():
        @pl.when(row == root)
        def _():
            for i in range(8):
                wait(MC.at[pl.ds(i, 1)], sem_c.at[i])
            for k in range(1, 4):
                remote(MC, MC, sem_cs.at[1 + k], sem_c.at[8], col, lax.rem(row + k, 4)).start()

    def wait_piv(s, i):
        wait(PV.at[s, pl.ds(128 * i, 128)], sem_p.at[s, i])
        A[pl.ds(128 * i, 128), pl.ds(128 * s, 128)] = PV[s, pl.ds(128 * i, 128), :].astype(F32)

    def widen():
        fetch.wait()

        @pl.loop(0, 12)
        def _(i):
            ACC[pl.ds(16 * i, 16)] = T[pl.ds(16 * i, 16)].astype(F32)

    dims = (((1,), (1,)), ((), ()))

    def product(m, half):
        acc = lax.dot_general(m, Z[:, half * HALF : half * HALF + HALF], dims, preferred_element_type=F32)
        return acc[:, 0:128] + acc[:, 128:256]

    def plane_y(dy):
        yy = wrap(y - dy, NY)
        at = [pl.ds((zz * NY + yy) * NX, 2) for zz in range(NZ)]
        m = jnp.concatenate([G[a] for a in at], axis=0).reshape(NZ * 64, HALF)
        d = product(m, 0).reshape(NZ * 2, 32, 128)
        for zz in range(NZ):
            ACC[at[zz]] -= d[2 * zz : 2 * zz + 2]

    def plane_z(dz):
        b = wrap(z - dz, NZ) * (NY * NX)
        m = G[pl.ds(NC + b, 16)].reshape(512, HALF)
        ACC[pl.ds(b, 16)] -= product(m, 1).reshape(16, 32, 128)

    near = max(t for t, (half, dz, dy, _), _ in events if half == 0 and dy == 0)
    todo = [(ev[0], 0, functools.partial(handle, ev)) for ev in events]
    todo += [(near + 0.01, 1, far_send), (near + 1.0, 2, widen), (near + 10.0, 3, far_relay)]
    begin, block = 4.0, 7.0
    solved = begin + 4 * block + 5.5
    planes = []
    for half, n, f in ((0, NY, plane_y), (1, NZ, plane_z)):
        for d in range(n):
            ready = max(ev[0] for ev in events if ev[1][0] == half and (ev[1][2 - half] - d) % n == 0)
            planes.append((ready, functools.partial(f, d)))
    planes.sort(key=lambda e: e[0])
    for i, (ready, f) in enumerate(planes):
        todo.append((max(ready + 0.01, solved + 0.4 * i), 4, f))
    todo.sort(key=lambda e: (e[0], e[1]))

    def run_until(t):
        while todo and todo[0][0] <= t:
            todo.pop(0)[2]()

    wait_piv(0, 0)
    for k in range(4):
        o = 128 * k

        def at(p):
            if p % (16 // POINTS) == 0:
                run_until(begin + block * (k + p / 16) - 0.3)

        D = A[o : o + 128, o : o + 128]
        Us, Vs = factor128([D[8 * p : 8 * p + 8] for p in range(16)], at)
        Vk = jnp.concatenate(Vs, axis=0)
        V[k] = Vk
        U[o : o + 128, o : o + 128] = jnp.concatenate(Us, axis=0)
        if k > 0:
            U[o : o + 128, 0:o] = jnp.zeros((128, o), F32)
        if k == 0:
            for s in range(1, 4):
                for i in range(s + 1):
                    wait_piv(s, i)
        if k < 3:
            rest = dot3(Vk, A[o : o + 128, o + 128 :], 1, 0)
            U[o : o + 128, o + 128 :] = rest
            for i in range(k + 1, 4):
                b = 128 * (i - k - 1)
                A[128 * i : 128 * i + 128, 128 * i :] -= dot3(rest[:, b : b + 128], rest[:, b:], 0, 0)

    run_until(begin + 4 * block)

    @pl.when(row != root)
    def _():
        wait(MC, sem_c.at[8])

    left = jnp.concatenate([MC[j] for j in range(4)] + [MS[0]], axis=0)
    right = jnp.concatenate([MC[4 + j] for j in range(4)] + [MS[1]], axis=0)
    rhs = [a[:, b : b + 128].astype(F32) for a in (left, right) for b in (0, 128)]
    for k in range(4):
        rhs[k] = dot3(rhs[k], V[k], 1, 1)
        for i in range(k + 1, 4):
            rhs[i] = rhs[i] - dot3(rhs[k], U[128 * k : 128 * k + 128, 128 * i : 128 * i + 128], 1, 0)
        p_ref[0, :, 128 * k : 128 * k + 128] = rhs[k][128:160].astype(BF)
        run_until(begin + 4 * block + 0.7 * (k + 1))
    back = [a[:128] for a in rhs]
    for k in range(3, -1, -1):
        zk = dot3(back[k], V[k], 1, 0)
        hi, lo = split(zk)
        Z[0:128, 128 * k : 128 * k + 128] = hi
        Z[128:256, 128 * k : 128 * k + 128] = lo
        for i in range(k):
            back[i] = back[i] - dot3(zk, U[128 * i : 128 * i + 128, 128 * k : 128 * k + 128], 1, 1)
        run_until(min(solved - 0.1, begin + 4 * block + 0.7 * (8 - k)))
    run_until(solved + 0.1)
    l_ref[...] = U[pl.ds(pl.multiple_of(row * 128, 128), 128), :].T
    run_until(1e9)

    outs = []
    for i in range(4):
        a = pl.ds(48 * i, 48)
        OUT[a] = ACC[a].astype(BF)
        outs.append(pltpu.make_async_copy(OUT.at[a], s_ref.at[a], sem_t.at[1 + i]))
        outs[i].start()

    for i, n in enumerate(sent):
        wait(G.at[pl.ds(0, n)], sem_s.at[i])
    for i in range(4):

        @pl.when(row >= i)
        def _():
            for k in range(1, 4):
                wait(piv_ref.at[pl.ds(128 * i, 128)], sem_ps.at[k - 1, i])

    @pl.when(goal != col)
    def _():
        for half in range(2):
            wait(MS.at[pl.ds(half, 1)], sem_cs.at[half])

    @pl.when(row == root)
    def _():
        for k in range(1, 4):
            wait(MC, sem_cs.at[1 + k])

    for c in outs:
        c.wait()


def body(pivot_block, panel, lead, trailing):
    start, events = plan()
    vm = pl.BlockSpec(memory_space=pltpu.VMEM)
    hbm = pl.BlockSpec(memory_space=pl.ANY)
    dma = pltpu.SemaphoreType.DMA
    schur, pf, lf = pl.pallas_call(
        step,
        out_shape=(
            jax.ShapeDtypeStruct((NC, 32, 128), BF),
            jax.ShapeDtypeStruct((1, 32, 512), BF),
            jax.ShapeDtypeStruct((512, 128), F32),
        ),
        in_specs=[vm, pl.BlockSpec(memory_space=pltpu.SMEM), vm, hbm],
        out_specs=(hbm, vm, vm),
        scratch_shapes=[
            pltpu.VMEM((2 * NC, 32, HALF), BF),
            pltpu.VMEM((NC, 32, 128), BF),
            pltpu.VMEM((NC, 32, 128), F32),
            pltpu.VMEM((NC, 32, 128), BF),
            pltpu.VMEM((512, 512), F32),
            pltpu.VMEM((256, 512), BF),
            pltpu.VMEM((4, 128, 128), F32),
            pltpu.VMEM((512, 512), F32),
            pltpu.VMEM((4, 512, 128), BF),
            pltpu.VMEM((2, 32, HALF), BF),
            pltpu.VMEM((8, 32, HALF), BF),
            dma((2,)),
            dma((2,)),
            dma((len(events) + 2 * len(start),)),
            dma((2,)),
            dma((2,)),
            dma((4, 4)),
            dma((3, 4)),
            dma((9,)),
            dma((5,)),
            dma((5,)),
        ],
        compiler_params=pltpu.CompilerParams(collective_id=0, has_side_effects=True, vmem_limit_bytes=67043328),
        name="cholesky_step",
    )(panel, lead, pivot_block, trailing.reshape(NC, 32, 128))
    return lf, pf, schur.reshape(6144, 128)


def solution(mesh):
    return jax.shard_map(
        body,
        mesh=mesh,
        in_specs=(P(None, "row"), P("row", "col", None), P("row", None), P("row", "col")),
        out_specs=(P(None, "row"), P("row", "col", None), P("row", "col")),
        check_vma=False,
    )
```

```python
import functools
import heapq

import jax
import jax.numpy as jnp
from jax import lax
from jax.experimental import pallas as pl
from jax.experimental.pallas import tpu as pltpu
from jax.sharding import PartitionSpec as P

F32 = jnp.float32
BF = jnp.bfloat16
MESH = pl.DeviceIdType.MESH
NZ, NY, NX, NR = 12, 8, 2, 4
NC = NZ * NY * NX
HALF = 256
POINTS = 16


def split(a):
    hi = a.astype(BF)
    return hi, (a - hi.astype(F32)).astype(BF)


def dot3(a, b, ca, cb):
    ah, al = split(a)
    bh, bl = split(b)
    d = functools.partial(
        lax.dot_general,
        dimension_numbers=(((ca,), (cb,)), ((), ())),
        preferred_element_type=F32,
    )
    return d(ah, bh) + (d(ah, bl) + d(al, bh))


def lane_b(x, j):
    return jnp.broadcast_to(x[:, j : j + 1], (8, 128))


def sub_b(x, i):
    return jnp.broadcast_to(x[i : i + 1, :], (8, 128))


def factor128(slabs, at):
    lane = lax.broadcasted_iota(jnp.int32, (8, 128), 1)
    sub = lax.broadcasted_iota(jnp.int32, (8, 128), 0)
    S = list(slabs)
    V = [jnp.where(lane == sub + 8 * p, F32(1.0), F32(0.0)) for p in range(16)]
    Us, Vs = [], []

    def gather_rows(rows):
        x = rows[0]
        for i in range(1, 8):
            x = jnp.where(sub == i, rows[i], x)
        return x

    for p in range(16):
        at(p)
        Sp, Vp = S[p], V[p]
        C = [lane_b(Sp, 8 * p + j) for j in range(8)]
        e = [[sub_b(C[j], i) for j in range(8)] for i in range(8)]
        r = [sub_b(Sp, i) for i in range(8)]
        v = [sub_b(Vp, i) for i in range(8)]
        d, ur, vr = [], [], []
        for j in range(8):
            inv = 1.0 / e[j][j]
            d.append(e[j][j])
            ur.append(r[j])
            vr.append(v[j])
            rj, vj = r[j] * inv, v[j] * inv
            ej = [e[j][m] * inv if m > j else None for m in range(8)]
            for i in range(8):
                if i != j:
                    f = e[i][j]
                    for m in range(j + 1, 8):
                        e[i][m] = e[i][m] - f * ej[m]
                    r[i] = r[i] - f * rj
                    v[i] = v[i] - f * vj
            r[j], v[j] = rj, vj
            for m in range(j + 1, 8):
                e[j][m] = ej[m]
        for q in range(p + 1, 16):
            T = [lane_b(S[q], 8 * p + j) for j in range(8)]
            a = [T[j] * r[j] for j in range(8)]
            b = [T[j] * v[j] for j in range(8)]
            while len(a) > 1:
                a = [a[i] + a[i + 1] for i in range(0, len(a), 2)]
                b = [b[i] + b[i + 1] for i in range(0, len(b), 2)]
            S[q] = S[q] - a[0]
            V[q] = V[q] - b[0]
        rs = lax.rsqrt(gather_rows(d))
        Us.append(jnp.where(lane >= sub + 8 * p, gather_rows(ur) * rs, F32(0.0)))
        Vs.append(gather_rows(vr) * rs)
    return Us, Vs


def reach(axis, sign, other):
    n = NZ if axis == "z" else NY
    return n // 2 if (other % 2 == 0) == (sign > 0) else n // 2 - 1


def plan():
    stages = {"z": 2, "y": 4}
    lag = {"z": 2.3, "y": 2.8, "x": 2.5}
    wire = 0.71

    def kind(half, dz, dy):
        far, side = (dy, dz) if half == 0 else (dz, dy)
        return "s" if far != 0 and abs(side) < 2 else "p"

    def children(half, dz, dy, k):
        if k == "x":
            return []
        last, first = ("y", "z") if half == 0 else ("z", "y")
        pos = {"z": dz, "y": dy}
        out = []

        def to(axis, new):
            q = dict(pos)
            q[axis] = new
            out.append((axis, new - pos[axis], (half, q["z"], q["y"], kind(half, q["z"], q["y"]))))

        if pos[last] == 0:
            here = pos[first]
            if here != 0 and abs(here) % stages[first] == 0:
                sign = 1 if here > 0 else -1
                for d in range(stages[first], 0, -1):
                    if abs(here) + d <= reach(first, sign, 0):
                        to(first, here + sign * d)
            for sign in (1, -1):
                to(last, sign)
        else:
            sign = 1 if pos[last] > 0 else -1
            if abs(pos[last]) + 1 <= reach(last, sign, pos[first]):
                to(last, pos[last] + sign)
        if k == "s":
            out.append(("x", 0, (half, dz, dy, "x")))
        return out

    free = {}
    heap = []
    order = []
    start = []
    count = 0

    def send(t, axis, delta, kid):
        nonlocal count
        w = wire if kid[3] == "p" else wire / 2
        key = (axis, delta > 0)
        begin = max(t, free.get(key, 0.0))
        free[key] = begin + w * max(1, abs(delta))
        heapq.heappush(heap, (begin + w + lag[axis] + 0.75 * max(0, abs(delta) - 1), count, kid))
        count += 1

    for d in range(4, 0, -1):
        for half, axis in ((0, "z"), (1, "y")):
            for sign in (1, -1):
                if d <= stages[axis] and d <= reach(axis, sign, 0):
                    kid = (0, sign * d, 0, "p") if axis == "z" else (1, 0, sign * d, "p")
                    start.append((axis, sign * d, kid))
                    send(0.0, axis, sign * d, kid)
    for half in range(2):
        heapq.heappush(heap, (3.0, count, (half, 0, 0, "p")))
        count += 1
    while heap:
        t, _, msg = heapq.heappop(heap)
        kids = children(*msg)
        order.append((t, msg, kids))
        for axis, delta, kid in kids:
            send(t, axis, delta, kid)
    return start, order


def step(
    x_ref, lead_ref, piv_ref, t_ref, s_ref, p_ref, l_ref,
    G, T, ACC, OUT, U, Z, V, A, PV, MS, MC,
    sem_xs, sem_xr, sem_r, sem_s, sem_l, sem_p, sem_ps, sem_c, sem_cs, sem_t,
):
    col, row = lax.axis_index("col"), lax.axis_index("row")
    z, y, x = col // (NY * NX), (col // NX) % NY, col % NX

    def wrap(v, n):
        return lax.rem(v + n, n)

    def away(axis, delta, xx):
        if axis == "x":
            return (z * NY + y) * NX + 1 - x
        if axis == "z":
            return (wrap(z + delta, NZ) * NY + y) * NX + xx
        return (z * NY + wrap(y + delta, NY)) * NX + xx

    def remote(src, dst, send, recv, c, r):
        return pltpu.make_async_remote_copy(
            src_ref=src, dst_ref=dst, send_sem=send, recv_sem=recv, device_id=(c, r), device_id_type=MESH
        )

    def wait(ref, sem):
        pltpu.make_async_copy(ref, ref, sem).wait()

    start, events = plan()
    barrier = pltpu.get_barrier_semaphore()
    targets = [(away("x", 0, x), row)]
    for xx in (x, 1 - x):
        targets += [(away("z", d, xx), row) for d in (-2, -1, 1, 2)]
        targets += [(away("y", d, xx), row) for d in (-3, -2, -1, 1, 2, 3, 4)]
    targets += [(col, lax.rem(row + k, 4)) for k in range(1, 4)]
    for t in targets:
        pl.semaphore_signal(barrier, inc=1, device_id=t, device_id_type=MESH)

    fetch = pltpu.make_async_copy(t_ref, T, sem_t.at[0])
    fetch.start()
    lane = lax.broadcasted_iota(jnp.int32, (32, HALF), 1)
    first = lead_ref[0, col // 4]
    for half in range(2):
        kept = (lane + half * HALF) // 128 >= first
        MS[half] = jnp.where(kept, x_ref[0, :, half * HALF : half * HALF + HALF].astype(F32), 0.0).astype(BF)
    for i in range(4):

        @pl.when(row >= i)
        def _():
            pltpu.make_async_copy(
                piv_ref.at[pl.ds(128 * i, 128)], PV.at[row, pl.ds(128 * i, 128)], sem_p.at[row, i]
            ).start()

    pl.semaphore_wait(barrier, len(targets))

    def send_piv(i):
        @pl.when(row >= i)
        def _():
            for k in range(1, 4):
                src, dst = piv_ref.at[pl.ds(128 * i, 128)], PV.at[row, pl.ds(128 * i, 128)]
                remote(src, dst, sem_ps.at[k - 1, i], sem_p.at[row, i], col, lax.rem(row + k, 4)).start()

    own, xs = [], []
    for half in range(2):
        dst = G.at[pl.ds(half * NC + col, 1)]
        xs.append(remote(MS.at[pl.ds(half, 1)], dst, sem_xs.at[half], sem_xr.at[half], away("x", 0, x), row))
        xs[half].start()
        own.append(pltpu.make_async_copy(MS.at[pl.ds(half, 1)], dst, sem_l.at[half]))
        own[half].start()
    send_piv(0)

    index = {msg: i for i, (_, msg, _) in enumerate(events)}
    both = {kid: i for i, (_, _, kid) in enumerate(start)}
    sent = [0]

    def send_sem(n):
        if sent[-1] + n > 2 * NC:
            sent.append(0)
        sent[-1] += n
        return sem_s.at[len(sent) - 1]

    for axis, delta, kid in start:
        src, dst = MS.at[pl.ds(kid[0], 1)], G.at[pl.ds(kid[0] * NC + col, 1)]
        for xx in (x, 1 - x):
            remote(src, dst, send_sem(1), sem_r.at[len(events) + 2 * both[kid] + x], away(axis, delta, xx), row).start()
    for i in range(1, 4):
        send_piv(i)

    def part(half, dz, dy, k):
        base = half * NC + (wrap(z - dz, NZ) * NY + wrap(y - dy, NY)) * NX
        if k == "p":
            return G.at[pl.ds(base, 2)]
        return G.at[pl.ds(base + (x if k == "s" else 1 - x), 1)]

    def handle(event):
        _, msg, kids = event
        half, dz, dy, k = msg
        ref = part(*msg)
        if dz == 0 and dy == 0:
            own[half].wait()
            xs[half].wait()
        elif msg in both:
            for q in range(2):
                wait(ref.at[pl.ds(q, 1)], sem_r.at[len(events) + 2 * both[msg] + q])
        else:
            wait(ref, sem_r.at[index[msg]])
        for axis, delta, kid in kids:
            pairs = k == "p" and kid[3] == "p"
            src = ref if pairs or k == "s" else part(half, dz, dy, "s")
            remote(src, src, send_sem(2 if pairs else 1), sem_r.at[index[kid]], away(axis, delta, x), row).start()

    goal = 48 * row + col // 4
    here = lax.rem(col, 4)

    def far_send():
        for half in range(2):
            src, dst = MS.at[pl.ds(half, 1)], MC.at[pl.ds(4 * half + here, 1)]

            @pl.when(goal != col)
            def _():
                remote(src, dst, sem_cs.at[half], sem_c.at[4 * half + here], goal, row).start()

            @pl.when(goal == col)
            def _():
                pltpu.make_async_copy(src, dst, sem_c.at[4 * half + here]).start()

    root = col // 48

    def far_relay():
        @pl.when(row == root)
        def _():
            for i in range(8):
                wait(MC.at[pl.ds(i, 1)], sem_c.at[i])
            for k in range(1, 4):
                remote(MC, MC, sem_cs.at[1 + k], sem_c.at[8], col, lax.rem(row + k, 4)).start()

    def wait_piv(s, i):
        wait(PV.at[s, pl.ds(128 * i, 128)], sem_p.at[s, i])
        A[pl.ds(128 * i, 128), pl.ds(128 * s, 128)] = PV[s, pl.ds(128 * i, 128), :].astype(F32)

    def widen():
        fetch.wait()

        @pl.loop(0, 12)
        def _(i):
            ACC[pl.ds(16 * i, 16)] = T[pl.ds(16 * i, 16)].astype(F32)

    dims = (((1,), (1,)), ((), ()))

    def product(m, half):
        acc = lax.dot_general(m, Z[:, half * HALF : half * HALF + HALF], dims, preferred_element_type=F32)
        return acc[:, 0:128] + acc[:, 128:256]

    def plane_y(dy):
        yy = wrap(y - dy, NY)
        at = [pl.ds((zz * NY + yy) * NX, 2) for zz in range(NZ)]
        m = jnp.concatenate([G[a] for a in at], axis=0).reshape(NZ * 64, HALF)
        d = product(m, 0).reshape(NZ * 2, 32, 128)
        for zz in range(NZ):
            ACC[at[zz]] -= d[2 * zz : 2 * zz + 2]

    def plane_z(dz):
        b = wrap(z - dz, NZ) * (NY * NX)
        m = G[pl.ds(NC + b, 16)].reshape(512, HALF)
        ACC[pl.ds(b, 16)] -= product(m, 1).reshape(16, 32, 128)

    near = max(t for t, (half, dz, dy, _), _ in events if half == 0 and dy == 0)
    todo = [(ev[0], 0, functools.partial(handle, ev)) for ev in events]
    todo += [(near + 0.01, 1, far_send), (near + 1.0, 2, widen), (near + 12.0, 3, far_relay)]
    begin, block = 4.0, 7.0
    solved = begin + 4 * block + 5.5
    planes = []
    for half, n, f in ((0, NY, plane_y), (1, NZ, plane_z)):
        for d in range(n):
            ready = max(ev[0] for ev in events if ev[1][0] == half and (ev[1][2 - half] - d) % n == 0)
            planes.append((ready, functools.partial(f, d)))
    planes.sort(key=lambda e: e[0])
    for i, (ready, f) in enumerate(planes):
        todo.append((max(ready + 0.01, solved + 0.4 * i), 4, f))
    todo.sort(key=lambda e: (e[0], e[1]))

    def run_until(t):
        while todo and todo[0][0] <= t:
            todo.pop(0)[2]()

    wait_piv(0, 0)
    for k in range(4):
        o = 128 * k

        def at(p):
            if p % (16 // POINTS) == 0:
                run_until(begin + block * (k + p / 16) - 0.3)

        D = A[o : o + 128, o : o + 128]
        Us, Vs = factor128([D[8 * p : 8 * p + 8] for p in range(16)], at)
        Vk = jnp.concatenate(Vs, axis=0)
        V[k] = Vk
        U[o : o + 128, o : o + 128] = jnp.concatenate(Us, axis=0)
        if k > 0:
            U[o : o + 128, 0:o] = jnp.zeros((128, o), F32)
        if k == 0:
            for s in range(1, 4):
                for i in range(s + 1):
                    wait_piv(s, i)
        if k < 3:
            rest = dot3(Vk, A[o : o + 128, o + 128 :], 1, 0)
            U[o : o + 128, o + 128 :] = rest
            for i in range(k + 1, 4):
                b = 128 * (i - k - 1)
                A[128 * i : 128 * i + 128, 128 * i :] -= dot3(rest[:, b : b + 128], rest[:, b:], 0, 0)

    run_until(begin + 4 * block)

    @pl.when(row != root)
    def _():
        wait(MC, sem_c.at[8])

    left = jnp.concatenate([MC[j] for j in range(4)] + [MS[0]], axis=0)
    right = jnp.concatenate([MC[4 + j] for j in range(4)] + [MS[1]], axis=0)
    rhs = [a[:, b : b + 128].astype(F32) for a in (left, right) for b in (0, 128)]
    for k in range(4):
        rhs[k] = dot3(rhs[k], V[k], 1, 1)
        for i in range(k + 1, 4):
            rhs[i] = rhs[i] - dot3(rhs[k], U[128 * k : 128 * k + 128, 128 * i : 128 * i + 128], 1, 0)
        p_ref[0, :, 128 * k : 128 * k + 128] = rhs[k][128:160].astype(BF)
        run_until(begin + 4 * block + 0.7 * (k + 1))
    back = [a[:128] for a in rhs]
    for k in range(3, -1, -1):
        zk = dot3(back[k], V[k], 1, 0)
        hi, lo = split(zk)
        Z[0:128, 128 * k : 128 * k + 128] = hi
        Z[128:256, 128 * k : 128 * k + 128] = lo
        for i in range(k):
            back[i] = back[i] - dot3(zk, U[128 * i : 128 * i + 128, 128 * k : 128 * k + 128], 1, 1)
        run_until(min(solved - 0.1, begin + 4 * block + 0.7 * (8 - k)))
    run_until(solved + 0.1)
    l_ref[...] = U[pl.ds(pl.multiple_of(row * 128, 128), 128), :].T
    run_until(1e9)

    outs = []
    for i in range(4):
        a = pl.ds(48 * i, 48)
        OUT[a] = ACC[a].astype(BF)
        outs.append(pltpu.make_async_copy(OUT.at[a], s_ref.at[a], sem_t.at[1 + i]))
        outs[i].start()

    for i, n in enumerate(sent):
        wait(G.at[pl.ds(0, n)], sem_s.at[i])
    for i in range(4):

        @pl.when(row >= i)
        def _():
            for k in range(1, 4):
                wait(piv_ref.at[pl.ds(128 * i, 128)], sem_ps.at[k - 1, i])

    @pl.when(goal != col)
    def _():
        for half in range(2):
            wait(MS.at[pl.ds(half, 1)], sem_cs.at[half])

    @pl.when(row == root)
    def _():
        for k in range(1, 4):
            wait(MC, sem_cs.at[1 + k])

    for c in outs:
        c.wait()


def body(pivot_block, panel, lead, trailing):
    start, events = plan()
    vm = pl.BlockSpec(memory_space=pltpu.VMEM)
    hbm = pl.BlockSpec(memory_space=pl.ANY)
    dma = pltpu.SemaphoreType.DMA
    schur, pf, lf = pl.pallas_call(
        step,
        out_shape=(
            jax.ShapeDtypeStruct((NC, 32, 128), BF),
            jax.ShapeDtypeStruct((1, 32, 512), BF),
            jax.ShapeDtypeStruct((512, 128), F32),
        ),
        in_specs=[vm, pl.BlockSpec(memory_space=pltpu.SMEM), vm, hbm],
        out_specs=(hbm, vm, vm),
        scratch_shapes=[
            pltpu.VMEM((2 * NC, 32, HALF), BF),
            pltpu.VMEM((NC, 32, 128), BF),
            pltpu.VMEM((NC, 32, 128), F32),
            pltpu.VMEM((NC, 32, 128), BF),
            pltpu.VMEM((512, 512), F32),
            pltpu.VMEM((256, 512), BF),
            pltpu.VMEM((4, 128, 128), F32),
            pltpu.VMEM((512, 512), F32),
            pltpu.VMEM((4, 512, 128), BF),
            pltpu.VMEM((2, 32, HALF), BF),
            pltpu.VMEM((8, 32, HALF), BF),
            dma((2,)),
            dma((2,)),
            dma((len(events) + 2 * len(start),)),
            dma((2,)),
            dma((2,)),
            dma((4, 4)),
            dma((3, 4)),
            dma((9,)),
            dma((5,)),
            dma((5,)),
        ],
        compiler_params=pltpu.CompilerParams(collective_id=0, has_side_effects=True, vmem_limit_bytes=67043328),
        name="cholesky_step",
    )(panel, lead, pivot_block, trailing.reshape(NC, 32, 128))
    return lf, pf, schur.reshape(6144, 128)


def solution(mesh):
    return jax.shard_map(
        body,
        mesh=mesh,
        in_specs=(P(None, "row"), P("row", "col", None), P("row", None), P("row", "col")),
        out_specs=(P(None, "row"), P("row", "col", None), P("row", "col")),
        check_vma=False,
    )
```
